32 devices in a mesh: dp: 8 (over z, x), tensor: 4 (over y, core).
Axes of the slice: x: 2, y: 2, z: 4, core: 2. Of those that a mesh axis runs over, the one named last changes fastest.
Arguments:
- queries: bfloat16 [8192, 1024], P('dp', 'tensor')
- keys: bfloat16 [8192, 1024], P('dp', 'tensor')
- values: bfloat16 [8192, 1024], P('dp', 'tensor'), may hold values from -6 to 6
- mem_keys: bfloat16 [16384, 1024], P('dp', 'tensor')
- mem_values: bfloat16 [16384, 1024], P('dp', 'tensor'), may hold values from -6 to 6
- gate_bias: float32 [8], P('tensor'), may hold values from -3 to 3
- out_weight: bfloat16 [1024, 7168], P('tensor'), may hold values from -0.25 to 0.25
- retrieved: int32 [64, 4], P('dp'), may hold values from 0 to 127, as said below
- block_slot: int32 [128], replicated, may hold values from 0 to 127, as said below
Outputs:
- mixed: bfloat16 [7168, 8192], P('tensor', 'dp')
The draws below stay inside these ranges and needn't reach their ends.
Inputs may be any that keep to these rules, and one draw needn't show every extreme that they name: Row b lists the 4 memory blocks retrieved for query block b, all different. Among the 32 entries of the rows of one device, at most 8 name blocks whose slots lie on one device (slot // 16), and these name at most 4 different blocks. `block_slot`: each slot once.
All inputs are finite; a program needn't handle non-finite values.
Results may differ from the reference program's by a relative error of at most 0.014.
Values may be sent and summed in bfloat16 or wider, within the bound.
A program may use at most 128 MiB of HBM per device.

```python
import jax
import jax.numpy as jnp
from jax import lax

D = 7168
HEAD = 128
HEADS_DEV = 2
BLOCK = 128
SEG = 512
TOPK = 4
REQ_CAP = 8
UNIQ_CAP = 4
TOK_DEV = 1024
MB_DEV = 16
TOKENS = 8192
QB_DEV = 8
NQB = 64
MEMBLOCKS = 128
MEMTOK = 16384
HEADS = 8
HD = 1024


def relabel(labels, first_value, second_value):
    return jnp.where(labels == first_value, second_value, jnp.where(labels == second_value, first_value, labels)).astype(jnp.int32)


def request_plan(key):
    base_key = jax.random.fold_in(key, 4101)
    subkeys = jax.random.split(base_key, 6)
    device_count = NQB // QB_DEV
    first_perm = jax.random.permutation(subkeys[0], MEMBLOCKS).astype(jnp.int32)
    block_at_slot = jnp.argsort(first_perm, stable=True).astype(jnp.int32)
    hot_owner = jax.random.randint(subkeys[1], (), 0, device_count).astype(jnp.int32)
    request_count = QB_DEV * TOPK
    rest_count = request_count - REQ_CAP
    other_owners = (hot_owner + 1 + jnp.arange(device_count - 1, dtype=jnp.int32)) % device_count
    owner_pool = jnp.repeat(other_owners, UNIQ_CAP)
    pool_length = (device_count - 1) * UNIQ_CAP
    shuffles = jax.vmap(lambda subkey: jax.random.permutation(subkey, pool_length))(jax.random.split(subkeys[2], device_count))
    picked_owners = owner_pool[shuffles[:, :rest_count]]
    owners = jnp.concatenate([jnp.full((device_count, REQ_CAP), hot_owner, jnp.int32), picked_owners.astype(jnp.int32)], axis=1)
    request_order = jnp.arange(request_count, dtype=jnp.int32)
    same_owner = owners[:, :, None] == owners[:, None, :]
    earlier = request_order[None, None, :] < request_order[None, :, None]
    owner_rank = jnp.sum(same_owner & earlier, axis=2).astype(jnp.int32)
    owner_rank = jnp.where(request_order[None, :] < REQ_CAP, request_order[None, :] // 2, owner_rank)
    spread = jax.random.randint(subkeys[3], (device_count, request_count), 0, MB_DEV // UNIQ_CAP).astype(jnp.int32)
    partner = jnp.where(request_order < REQ_CAP, request_order // 2 * 2, request_order)
    spread = spread[:, partner]
    local_slot = owner_rank + UNIQ_CAP * spread
    global_slot = owners * MB_DEV + local_slot
    first_label = block_at_slot[global_slot[0, 0]]
    block_at_slot = relabel(block_at_slot, first_label, 0)
    last_label = block_at_slot[global_slot[0, 2]]
    block_at_slot = relabel(block_at_slot, last_label, MEMBLOCKS - 1)
    slot_of_block = jnp.argsort(block_at_slot, stable=True).astype(jnp.int32)
    block_ids = block_at_slot[global_slot]
    block_perm = jax.vmap(lambda subkey: jax.random.permutation(subkey, QB_DEV))(jax.random.split(subkeys[4], device_count)).astype(jnp.int32)
    rotation = jax.random.randint(subkeys[5], (device_count, QB_DEV), 0, TOPK).astype(jnp.int32)
    query_block = block_perm[:, request_order % QB_DEV]
    column = (request_order[None, :] // QB_DEV + jnp.take_along_axis(rotation, query_block, axis=1)) % TOPK
    device_rows = jnp.broadcast_to(jnp.arange(device_count, dtype=jnp.int32)[:, None], (device_count, request_count))
    placed = jnp.zeros((device_count, QB_DEV, TOPK), jnp.int32).at[device_rows, query_block, column].set(block_ids)
    return (placed.reshape(NQB, TOPK), slot_of_block)


def draw_retrieved(key, part):
    return request_plan(key)[0]


def draw_block_slot(key, part):
    return request_plan(key)[1]


def draw_queries(key, part):
    base_rows = jax.random.normal(jax.random.fold_in(key, 11), (TOKENS, HD), jnp.float32)
    return base_rows.astype(jnp.bfloat16)


def draw_keys(key, part):
    base_rows = jax.random.normal(jax.random.fold_in(key, 31), (TOKENS, HD), jnp.float32)
    return base_rows.astype(jnp.bfloat16)


def draw_mem_keys(key, part):
    base_rows = jax.random.normal(jax.random.fold_in(key, 41), (MEMTOK, HD), jnp.float32)
    return base_rows.astype(jnp.bfloat16)


def raised(array, stream_key, source, target, blocks, factor):
    def block_of(position):
        return (jnp.arange(array.shape[position]) // (array.shape[position] // blocks)).reshape((-1,) + (1,) * (array.ndim - 1 - position))

    first = jax.random.permutation(stream_key, blocks)[block_of(target)]
    far = (block_of(target) + blocks // 2) % blocks
    return jnp.where((block_of(source) == first) | (block_of(source) == far), factor * array, array)


def levels(rng, dims, shards, least, high):
    factor_of = 1.0
    for dim, shards_of in shards:
        heights = jax.random.uniform(jax.random.fold_in(jax.random.fold_in(rng, 6), dim), (shards_of,), jnp.float32, least / len(shards), high / len(shards))
        factor_of = factor_of * jnp.repeat(jnp.exp(heights), dims[dim] // shards_of).reshape((-1,) + (1,) * (len(dims) - 1 - dim))
    return factor_of


def bell_draw(stream_key, extent, width, bound, cuts=(), kind=jnp.bfloat16):
    factor_of = levels(stream_key, extent, cuts, -0.22, 0.18) if cuts else 1.0
    values = jax.random.normal(stream_key, extent, jnp.float32) * width * factor_of
    return jnp.minimum(jnp.maximum(values, -bound), bound).astype(kind)


def gaussian_with(stream_key, shape, scale, most, pieces, heavy, kind=jnp.bfloat16):
    result = scale * jax.random.normal(stream_key, shape, jnp.float32)
    if pieces:
        result = result * levels(stream_key, shape, pieces, -0.22, 0.18)
    return jnp.clip(raised(result, jax.random.fold_in(stream_key, 3), *heavy), -most, most).astype(kind)


def setup_inputs(seed: int = 0) -> dict:
    splits = jax.random.split(jax.random.key(seed), 10)
    queries = draw_queries(jax.random.fold_in(splits[9], 71), 0)
    keys = draw_keys(jax.random.fold_in(splits[9], 71), 0)
    values = bell_draw(splits[2], (TOKENS, HD), 1.0, 6.0, ((0, 8), (1, 4)))
    mem_keys = draw_mem_keys(jax.random.fold_in(splits[9], 71), 0)
    mem_values = bell_draw(splits[4], (MEMTOK, HD), 1.0, 6.0, ((0, 8), (1, 4)))
    gate_bias = jnp.clip(jax.random.uniform(splits[5], (HEADS,), jnp.float32, -3.0, 3.0) * levels(splits[5], (HEADS,), ((0, 4),), -0.4, 0.0), -3.0, 3.0)
    out_weight = gaussian_with(splits[6], (HD, D), HD ** -0.5, 0.25, ((0, 4),), (0, 1, 4, 2.0))
    retrieved = draw_retrieved(jax.random.fold_in(splits[9], 71), 0)
    block_slot = draw_block_slot(jax.random.fold_in(splits[9], 71), 0)
    return {"queries": queries, "keys": keys, "values": values, "mem_keys": mem_keys, "mem_values": mem_values, "gate_bias": gate_bias, "out_weight": out_weight, "retrieved": retrieved, "block_slot": block_slot}


def attend(query_rows, key_rows, value_rows, causal):
    scores = jnp.einsum("qhd,khd->hqk", query_rows.astype(jnp.float32), key_rows.astype(jnp.float32)) * (HEAD ** -0.5)
    if causal:
        causal_mask = jnp.arange(query_rows.shape[0])[:, None] >= jnp.arange(key_rows.shape[0])[None, :]
        scores = jnp.where(causal_mask[None, :, :], scores, -jnp.inf)
    weights = jax.nn.softmax(scores, axis=-1).astype(jnp.bfloat16)
    return jnp.einsum("hqk,khd->qhd", weights.astype(jnp.float32), value_rows.astype(jnp.float32))


def reference(queries, keys, values, mem_keys, mem_values, gate_bias, out_weight, retrieved, block_slot):
    seg_count = TOKENS // SEG
    seg_shape = (seg_count, SEG, HEADS, HEAD)

    def local_segment(triple_rows):
        return attend(triple_rows[0], triple_rows[1], triple_rows[2], True)

    local_out = lax.map(local_segment, (queries.reshape(seg_shape), keys.reshape(seg_shape), values.reshape(seg_shape)))
    local_out = local_out.reshape(TOKENS, HEADS, HEAD)

    memory_keys = mem_keys.reshape(MEMBLOCKS, BLOCK, HEADS, HEAD)
    memory_values = mem_values.reshape(MEMBLOCKS, BLOCK, HEADS, HEAD)
    slot_lists = block_slot[retrieved].astype(jnp.int32)

    def memory_block(block_pair):
        query_rows, slot_row = block_pair
        key_rows = memory_keys[slot_row].reshape(TOPK * BLOCK, HEADS, HEAD)
        value_rows = memory_values[slot_row].reshape(TOPK * BLOCK, HEADS, HEAD)
        return attend(query_rows, key_rows, value_rows, False)

    mem_out = lax.map(memory_block, (queries.reshape(NQB, BLOCK, HEADS, HEAD), slot_lists))
    mem_out = mem_out.reshape(TOKENS, HEADS, HEAD)

    mem_gate = jax.nn.sigmoid(gate_bias.astype(jnp.float32))[None, :, None]
    attended = (mem_gate * mem_out + (1.0 - mem_gate) * local_out).astype(jnp.bfloat16).reshape(TOKENS, HD)

    group_count = HEADS // HEADS_DEV
    group_width = HEADS_DEV * HEAD
    weight_groups = out_weight.reshape(group_count, group_width, D)

    def project(token_rows):
        group_rows = token_rows.reshape(TOK_DEV, group_count, group_width).transpose(1, 0, 2)

        def add_group(running, group_pair):
            partial_value = jnp.dot(group_pair[0], group_pair[1], preferred_element_type=jnp.float32).astype(jnp.bfloat16)
            partial_value = lax.optimization_barrier(partial_value)
            return running + partial_value.astype(jnp.float32), None

        running, unused = lax.scan(add_group, jnp.zeros((TOK_DEV, D), jnp.float32), (group_rows, weight_groups))
        return running.astype(jnp.bfloat16)

    mixed = lax.map(project, attended.reshape(TOKENS // TOK_DEV, TOK_DEV, HD)).reshape(TOKENS, D)
    return mixed.T
```

```python
import functools
import math

import jax
import jax.numpy as jnp
from jax import lax
from jax.experimental import pallas as pl
from jax.experimental.pallas import tpu as pltpu
from jax.sharding import PartitionSpec as P

BLOCK = 128
SEG = 512
TOPK = 4
UNIQ_CAP = 4
MESH = pl.DeviceIdType.MESH
NT = (((1,), (1,)), ((), ()))


def flipped(index, mask):
    bit = 1
    result = index
    while bit <= mask:
        if mask & bit:
            result = result + bit * (1 - 2 * (lax.rem(lax.div(index, bit), 2)))
        bit *= 2
    return result


def layer_kernel(
    peers, groups, heads, sliced,
    place_ref, req_ref, gate_ref, q_hbm, k_hbm, v_hbm, mk_hbm, mv_hbm, w_hbm,
    ag_hbm, wg_hbm,
    q_vm, k_vm, v_vm, mk_vm, mv_vm, req_in, req_sm, send_k, send_v, recv_k, recv_v,
    probs, coef, local, att,
    in_sem, smem_sem, own_sem, req_ss, req_rs, k_ss, k_rs, v_ss, v_rs, w_ss, w_rs,
    a_ss, a_rs, f_ss, f_rs,
):
    me = lax.axis_index("dp")
    tme = lax.axis_index("tensor")
    tok, width = q_vm.shape
    head = width // heads
    feats = wg_hbm.shape[1]
    scale = head ** -0.5 * math.log2(math.e)
    chunks = a_ss.shape[0]
    crow = tok // chunks

    loads = [
        pltpu.make_async_copy(src, dst, in_sem.at[i])
        for i, (src, dst) in enumerate(
            ((mk_hbm, mk_vm), (mv_hbm, mv_vm), (q_hbm, q_vm), (k_hbm, k_vm), (v_hbm, v_vm))
        )
    ]
    for load in loads:
        load.start()

    barrier = pltpu.get_barrier_semaphore()
    for m in range(1, peers):
        pl.semaphore_signal(barrier, inc=1, device_id={"dp": flipped(me, m)}, device_id_type=MESH)
    for m in range(1, groups):
        pl.semaphore_signal(
            barrier, inc=1, device_id={"tensor": flipped(tme, m)}, device_id_type=MESH
        )
    pl.semaphore_wait(barrier, peers - 1 + groups - 1)

    order = list(range(peers // 2, peers)) + list(range(peers // 2 - 1, 0, -1))

    req_copies = []
    for m in order:
        peer = flipped(me, m)
        copy = pltpu.make_async_remote_copy(
            src_ref=req_ref.at[peer], dst_ref=req_in.at[m], send_sem=req_ss.at[m],
            recv_sem=req_rs.at[m], device_id={"dp": peer}, device_id_type=MESH,
        )
        copy.start()
        req_copies.append(copy)

    def weight_part(t):
        if sliced:
            return w_hbm.at[:, pl.ds(pl.multiple_of(t * feats, 128), feats)]
        return w_hbm.at[t]

    def weight_place(t):
        return wg_hbm.at[pl.ds(pl.multiple_of(t * width, 128), width)]

    w_copies = []
    for m in range(1, groups):
        peer = flipped(tme, m)
        copy = pltpu.make_async_remote_copy(
            src_ref=weight_part(peer), dst_ref=weight_place(tme), send_sem=w_ss.at[m],
            recv_sem=w_rs.at[m], device_id={"tensor": peer}, device_id_type=MESH,
        )
        copy.start()
        w_copies.append(copy)
    own_w = pltpu.make_async_copy(weight_part(tme), weight_place(tme), own_sem.at[0])
    own_w.start()

    own_req = pltpu.make_async_copy(req_ref.at[me], req_in.at[0], own_sem.at[1])
    own_req.start()
    own_req.wait()
    for copy in req_copies:
        copy.wait()
    to_smem = pltpu.make_async_copy(req_in, req_sm, smem_sem)
    to_smem.start()
    loads[0].wait()
    to_smem.wait()

    def ship(source, send, recv, ss, rs):
        copies = []
        for m in order:
            peer = flipped(me, m)
            for c in range(UNIQ_CAP):
                send[m, c] = source[req_sm[m, 0, c]]
            copy = pltpu.make_async_remote_copy(
                src_ref=send.at[m], dst_ref=recv.at[me], send_sem=ss.at[m],
                recv_sem=rs.at[m], device_id={"dp": peer}, device_id_type=MESH,
            )
            copy.start()
            copies.append(copy)
        for c in range(UNIQ_CAP):
            recv[me, c] = source[req_sm[0, 0, c]]
        return copies

    k_copies = ship(mk_vm, send_k, recv_k, k_ss, k_rs)
    loads[1].wait()
    v_copies = ship(mv_vm, send_v, recv_v, v_ss, v_rs)
    for load in loads[2:]:
        load.wait()

    blocks_seg = SEG // BLOCK

    def local_segment(s, carry):
        base = pl.multiple_of(s * SEG, SEG)
        for h in range(heads):
            cols = slice(h * head, (h + 1) * head)
            gate = gate_ref[:, cols]
            for i in range(blocks_seg):
                span = (i + 1) * BLOCK
                rows = pl.ds(pl.multiple_of(base + i * BLOCK, BLOCK), BLOCK)
                scores = lax.dot_general(
                    q_vm[rows, cols], k_vm[pl.ds(base, span), cols], NT,
                    preferred_element_type=jnp.float32,
                )
                row = lax.broadcasted_iota(jnp.int32, (BLOCK, span), 0) + i * BLOCK
                col = lax.broadcasted_iota(jnp.int32, (BLOCK, span), 1)
                scores = jnp.where(col <= row, scores, -jnp.inf)
                top = jnp.max(scores, axis=1, keepdims=True)
                weights = jnp.exp2((scores - top) * scale)
                total = jnp.sum(weights, axis=1, keepdims=True)
                out = jnp.dot(
                    weights.astype(jnp.bfloat16), v_vm[pl.ds(base, span), cols],
                    preferred_element_type=jnp.float32,
                )
                local[rows, cols] = out * ((1.0 - gate) / total)
        return carry

    lax.fori_loop(0, tok // SEG, local_segment, 0)

    for copy in k_copies:
        copy.wait_recv()

    def mem_scores(b, carry):
        rows = pl.ds(pl.multiple_of(b * BLOCK, BLOCK), BLOCK)
        found = [
            recv_k[place_ref[0, b * TOPK + j], place_ref[1, b * TOPK + j]] for j in range(TOPK)
        ]
        for h in range(heads):
            cols = slice(h * head, (h + 1) * head)
            keys = jnp.concatenate([block[:, cols] for block in found], axis=0)
            scores = lax.dot_general(
                q_vm[rows, cols], keys, NT, preferred_element_type=jnp.float32
            )
            top = jnp.max(scores, axis=1, keepdims=True)
            weights = jnp.exp2((scores - top) * scale)
            total = jnp.sum(weights, axis=1, keepdims=True)
            probs[b, h] = weights.astype(jnp.bfloat16)
            coef[rows, cols] = gate_ref[:, cols] / total
        return carry

    lax.fori_loop(0, tok // BLOCK, mem_scores, 0)

    for copy in v_copies:
        copy.wait_recv()

    def mem_values(b, carry):
        rows = pl.ds(pl.multiple_of(b * BLOCK, BLOCK), BLOCK)
        found = [
            recv_v[place_ref[0, b * TOPK + j], place_ref[1, b * TOPK + j]] for j in range(TOPK)
        ]
        for h in range(heads):
            cols = slice(h * head, (h + 1) * head)
            vals = jnp.concatenate([block[:, cols] for block in found], axis=0)
            out = jnp.dot(probs[b, h], vals, preferred_element_type=jnp.float32)
            att[rows, cols] = (coef[rows, cols] * out + local[rows, cols]).astype(att.dtype)
        return carry

    def att_place(t, c):
        return ag_hbm.at[
            pl.ds(c * crow, crow), pl.ds(pl.multiple_of(t * width, 128), width)
        ]

    mate = flipped(tme, 1)
    others = list(range(2, groups, 2))
    a_copies = {}
    own_copies = [own_w]
    for c in range(chunks):
        lax.fori_loop(c * crow // BLOCK, (c + 1) * crow // BLOCK, mem_values, 0)
        mine = att.at[pl.ds(c * crow, crow)]
        for m in others + [1]:
            copy = pltpu.make_async_remote_copy(
                src_ref=mine, dst_ref=att_place(tme, c), send_sem=a_ss.at[c, m],
                recv_sem=a_rs.at[c, m], device_id={"tensor": flipped(tme, m)},
                device_id_type=MESH,
            )
            copy.start()
            a_copies[c, m] = copy
        own = pltpu.make_async_copy(mine, att_place(tme, c), own_sem.at[2 + c])
        own.start()
        own_copies.append(own)

    f_copies = []
    for c in range(chunks):
        for m in others:
            a_copies[c, m].wait_recv()
            part = att_place(flipped(tme, m), c)
            copy = pltpu.make_async_remote_copy(
                src_ref=part, dst_ref=part, send_sem=f_ss.at[c, m], recv_sem=f_rs.at[c, m],
                device_id={"tensor": mate}, device_id_type=MESH,
            )
            copy.start()
            f_copies.append(copy)
    for c in range(chunks):
        a_copies[c, 1].wait_recv()
    for copy in f_copies:
        copy.wait()
    for copy in a_copies.values():
        copy.wait_send()
    for copy in w_copies:
        copy.wait()
    for copy in k_copies + v_copies:
        copy.wait_send()
    for copy in own_copies:
        copy.wait()


def request_plan(retrieved, block_slot, local_blocks, peer_count):
    wanted = retrieved.reshape(-1)
    count = wanted.shape[0]
    table_ids = jnp.arange(block_slot.shape[0], dtype=jnp.int32)
    slot = jnp.sum(
        jnp.where(wanted[:, None] == table_ids[None, :], block_slot[None, :], 0), axis=1
    )
    owner = slot // local_blocks
    number = jnp.arange(count, dtype=jnp.int32)
    same = slot[:, None] == slot[None, :]
    first = jnp.min(jnp.where(same, number[None, :], count), axis=1)
    leads = first == number
    before = (
        leads[None, :] & (owner[:, None] == owner[None, :]) & (number[None, :] < first[:, None])
    )
    position = jnp.sum(before.astype(jnp.int32), axis=1)
    peer_ids = jnp.arange(peer_count, dtype=jnp.int32)
    lanes = jnp.arange(128, dtype=jnp.int32)
    match = (owner[:, None, None] == peer_ids[None, :, None]) & (
        position[:, None, None] == lanes[None, None, :]
    )
    request = jnp.max(jnp.where(match, (slot % local_blocks)[:, None, None], 0), axis=0)
    return jnp.stack([owner, position]), request


def shards(
    queries, keys, values, mem_keys, mem_values, gate_bias, out_weight, retrieved, block_slot
):
    tok, width = queries.shape
    heads = gate_bias.shape[0]
    head = width // heads
    peers = lax.axis_size("dp")
    groups = lax.axis_size("tensor")
    local_blocks = mem_keys.shape[0] // BLOCK
    feats = out_weight.shape[1] // groups
    chunks = tok // 256
    place, request = request_plan(retrieved, block_slot, local_blocks, peers)
    request = jnp.broadcast_to(request[:, None, :], (peers, 8, 128))
    gate_row = jnp.repeat(jax.nn.sigmoid(gate_bias), head)[None, :]
    sliced = feats % 128 == 0
    weight = out_weight
    if not sliced:
        weight = out_weight.reshape(width, groups, feats).transpose(1, 0, 2)
    blocked = (local_blocks, BLOCK, width)
    bf16 = jnp.bfloat16
    dma = pltpu.SemaphoreType.DMA
    any_spec = pl.BlockSpec(memory_space=pl.ANY)
    gathered, weights = pl.pallas_call(
        functools.partial(layer_kernel, peers, groups, heads, sliced),
        out_shape=(
            jax.ShapeDtypeStruct((tok, groups * width), bf16),
            jax.ShapeDtypeStruct((groups * width, feats), bf16),
        ),
        in_specs=[
            pl.BlockSpec(memory_space=pltpu.SMEM),
            pl.BlockSpec(memory_space=pltpu.VMEM),
            pl.BlockSpec(memory_space=pltpu.VMEM),
        ]
        + [any_spec] * 6,
        out_specs=(any_spec, any_spec),
        scratch_shapes=[
            pltpu.VMEM((tok, width), bf16),
            pltpu.VMEM((tok, width), bf16),
            pltpu.VMEM((tok, width), bf16),
            pltpu.VMEM(blocked, bf16),
            pltpu.VMEM(blocked, bf16),
            pltpu.VMEM((peers, 8, 128), jnp.int32),
            pltpu.SMEM((peers, 8, 128), jnp.int32),
            pltpu.VMEM((peers, UNIQ_CAP, BLOCK, width), bf16),
            pltpu.VMEM((peers, UNIQ_CAP, BLOCK, width), bf16),
            pltpu.VMEM((peers, UNIQ_CAP, BLOCK, width), bf16),
            pltpu.VMEM((peers, UNIQ_CAP, BLOCK, width), bf16),
            pltpu.VMEM((tok // BLOCK, heads, BLOCK, TOPK * BLOCK), bf16),
            pltpu.VMEM((tok, width), jnp.float32),
            pltpu.VMEM((tok, width), jnp.float32),
            pltpu.VMEM((tok, width), bf16),
            dma((5,)),
            dma(()),
            dma((2 + chunks,)),
            dma((peers,)),
            dma((peers,)),
            dma((peers,)),
            dma((peers,)),
            dma((peers,)),
            dma((peers,)),
            dma((groups,)),
            dma((groups,)),
            dma((chunks, groups)),
            dma((chunks, groups)),
            dma((chunks, groups)),
            dma((chunks, groups)),
        ],
        compiler_params=pltpu.CompilerParams(
            collective_id=0, has_side_effects=True, vmem_limit_bytes=52 * 2**20
        ),
        name="memory_layer",
    )(
        place, request, gate_row, queries, keys, values,
        mem_keys.reshape(blocked), mem_values.reshape(blocked), weight,
    )
    return lax.dot_general(
        weights, gathered, (((0,), (1,)), ((), ())), preferred_element_type=jnp.float32
    ).astype(bf16)


def solution(mesh):
    in_specs = (
        P("dp", "tensor"),
        P("dp", "tensor"),
        P("dp", "tensor"),
        P("dp", "tensor"),
        P("dp", "tensor"),
        P("tensor"),
        P("tensor", None),
        P("dp", None),
        P(),
    )
    out_specs = P("tensor", "dp")
    return jax.shard_map(shards, mesh=mesh, in_specs=in_specs, out_specs=out_specs, check_vma=False)
```

```python
import functools
import math

import jax
import jax.numpy as jnp
from jax import lax
from jax.experimental import pallas as pl
from jax.experimental.pallas import tpu as pltpu
from jax.sharding import PartitionSpec as P

BLOCK = 128
SEG = 512
TOPK = 4
UNIQ_CAP = 4
MESH = pl.DeviceIdType.MESH
NT = (((1,), (1,)), ((), ()))


def flipped(index, mask):
    bit = 1
    result = index
    while bit <= mask:
        if mask & bit:
            result = result + bit * (1 - 2 * (lax.rem(lax.div(index, bit), 2)))
        bit *= 2
    return result


def layer_kernel(
    peers, groups, heads, sliced,
    place_ref, req_ref, gate_ref, q_hbm, k_hbm, v_hbm, mk_hbm, mv_hbm, w_hbm,
    ag_hbm, wg_hbm,
    q_vm, k_vm, v_vm, mk_vm, mv_vm, req_in, req_sm, send_k, send_v, recv_k, recv_v,
    probs, coef, local, att,
    in_sem, smem_sem, own_sem, req_ss, req_rs, k_ss, k_rs, v_ss, v_rs, w_ss, w_rs,
    a_ss, a_rs, f_ss, f_rs,
):
    me = lax.axis_index("dp")
    tme = lax.axis_index("tensor")
    tok, width = q_vm.shape
    head = width // heads
    feats = wg_hbm.shape[1]
    scale = head ** -0.5 * math.log2(math.e)
    chunks = a_ss.shape[1]
    crow = tok // chunks

    loads = [
        pltpu.make_async_copy(src, dst, in_sem.at[i])
        for i, (src, dst) in enumerate(
            ((mk_hbm, mk_vm), (mv_hbm, mv_vm), (q_hbm, q_vm), (k_hbm, k_vm), (v_hbm, v_vm))
        )
    ]
    for load in loads:
        load.start()

    barrier = pltpu.get_barrier_semaphore()
    for m in range(1, peers):
        pl.semaphore_signal(barrier, inc=1, device_id={"dp": flipped(me, m)}, device_id_type=MESH)
    for m in range(1, groups):
        pl.semaphore_signal(
            barrier, inc=1, device_id={"tensor": flipped(tme, m)}, device_id_type=MESH
        )
    pl.semaphore_wait(barrier, peers - 1 + groups - 1)

    order = list(range(peers // 2, peers)) + list(range(peers // 2 - 1, 0, -1))

    req_copies = []
    for m in order:
        peer = flipped(me, m)
        copy = pltpu.make_async_remote_copy(
            src_ref=req_ref.at[peer], dst_ref=req_in.at[m], send_sem=req_ss.at[m],
            recv_sem=req_rs.at[m], device_id={"dp": peer}, device_id_type=MESH,
        )
        copy.start()
        req_copies.append(copy)

    def weight_part(t):
        if sliced:
            return w_hbm.at[:, pl.ds(pl.multiple_of(t * feats, 128), feats)]
        return w_hbm.at[t]

    def weight_place(t):
        return wg_hbm.at[pl.ds(pl.multiple_of(t * width, 128), width)]

    w_copies = []
    for m in range(1, groups):
        peer = flipped(tme, m)
        copy = pltpu.make_async_remote_copy(
            src_ref=weight_part(peer), dst_ref=weight_place(tme), send_sem=w_ss.at[m],
            recv_sem=w_rs.at[m], device_id={"tensor": peer}, device_id_type=MESH,
        )
        copy.start()
        w_copies.append(copy)
    own_w = pltpu.make_async_copy(weight_part(tme), weight_place(tme), own_sem.at[0])
    own_w.start()

    own_req = pltpu.make_async_copy(req_ref.at[me], req_in.at[0], own_sem.at[1])
    own_req.start()
    own_req.wait()
    for copy in req_copies:
        copy.wait()
    to_smem = pltpu.make_async_copy(req_in, req_sm, smem_sem)
    to_smem.start()
    loads[0].wait()
    to_smem.wait()

    def ship(source, h, send, recv, ss, rs):
        copies = []
        cols = slice(h * head, (h + 1) * head)
        for m in order:
            peer = flipped(me, m)
            for c in range(UNIQ_CAP):
                send[h, m, c] = source[req_sm[m, 0, c], :, cols]
            copy = pltpu.make_async_remote_copy(
                src_ref=send.at[h, m], dst_ref=recv[h].at[me], send_sem=ss.at[h, m],
                recv_sem=rs.at[h, m], device_id={"dp": peer}, device_id_type=MESH,
            )
            copy.start()
            copies.append(copy)
        for c in range(UNIQ_CAP):
            recv[h][me, c] = source[req_sm[0, 0, c], :, cols]
        return copies

    k_copies, v_copies = [], []
    for h in range(heads):
        k_copies.append(ship(mk_vm, h, send_k, recv_k, k_ss, k_rs))
        if h == 0:
            loads[1].wait()
        v_copies.append(ship(mv_vm, h, send_v, recv_v, v_ss, v_rs))
    for load in loads[2:]:
        load.wait()

    blocks_seg = SEG // BLOCK

    def local_segment(s, carry):
        base = pl.multiple_of(s * SEG, SEG)
        for h in range(heads):
            cols = slice(h * head, (h + 1) * head)
            gate = gate_ref[:, cols]
            for i in range(blocks_seg):
                span = (i + 1) * BLOCK
                rows = pl.ds(pl.multiple_of(base + i * BLOCK, BLOCK), BLOCK)
                scores = lax.dot_general(
                    q_vm[rows, cols], k_vm[pl.ds(base, span), cols], NT,
                    preferred_element_type=jnp.float32,
                )
                row = lax.broadcasted_iota(jnp.int32, (BLOCK, span), 0) + i * BLOCK
                col = lax.broadcasted_iota(jnp.int32, (BLOCK, span), 1)
                scores = jnp.where(col <= row, scores, -jnp.inf)
                top = jnp.max(scores, axis=1, keepdims=True)
                weights = jnp.exp2((scores - top) * scale)
                total = jnp.sum(weights, axis=1, keepdims=True)
                out = jnp.dot(
                    weights.astype(jnp.bfloat16), v_vm[pl.ds(base, span), cols],
                    preferred_element_type=jnp.float32,
                )
                local[rows, cols] = out * ((1.0 - gate) / total)
        return carry

    lax.fori_loop(0, tok // SEG, local_segment, 0)

    def fetched(recv, h, b):
        return jnp.concatenate(
            [
                recv[h][place_ref[0, b * TOPK + j], place_ref[1, b * TOPK + j]]
                for j in range(TOPK)
            ],
            axis=0,
        )

    def mem_scores(h, b, carry):
        rows = pl.ds(pl.multiple_of(b * BLOCK, BLOCK), BLOCK)
        cols = slice(h * head, (h + 1) * head)
        scores = lax.dot_general(
            q_vm[rows, cols], fetched(recv_k, h, b), NT, preferred_element_type=jnp.float32
        )
        top = jnp.max(scores, axis=1, keepdims=True)
        weights = jnp.exp2((scores - top) * scale)
        total = jnp.sum(weights, axis=1, keepdims=True)
        probs[b] = weights.astype(jnp.bfloat16)
        coef[rows, :] = gate_ref[:, cols] / total
        return carry

    def mem_values(h, b, carry):
        rows = pl.ds(pl.multiple_of(b * BLOCK, BLOCK), BLOCK)
        cols = slice(h * head, (h + 1) * head)
        out = jnp.dot(probs[b], fetched(recv_v, h, b), preferred_element_type=jnp.float32)
        att[h, rows, :] = (coef[rows, :] * out + local[rows, cols]).astype(att.dtype)
        return carry

    def att_place(t, h, c):
        column = pl.multiple_of(t * width + h * head, 128)
        return ag_hbm.at[pl.ds(c * crow, crow), pl.ds(column, head)]

    mate = flipped(tme, 1)
    others = list(range(2, groups, 2))
    a_copies, f_copies = {}, []
    own_copies = [own_w]

    def forward(h):
        for c in range(chunks):
            for m in others:
                a_copies[h, c, m].wait_recv()
                part = att_place(flipped(tme, m), h, c)
                copy = pltpu.make_async_remote_copy(
                    src_ref=part, dst_ref=part, send_sem=f_ss.at[h, c, m],
                    recv_sem=f_rs.at[h, c, m], device_id={"tensor": mate}, device_id_type=MESH,
                )
                copy.start()
                f_copies.append(copy)

    for h in range(heads):
        for copy in k_copies[h]:
            copy.wait_recv()
        lax.fori_loop(0, tok // BLOCK, functools.partial(mem_scores, h), 0)
        if h > 0:
            forward(h - 1)
        for copy in v_copies[h]:
            copy.wait_recv()
        for c in range(chunks):
            lax.fori_loop(
                c * crow // BLOCK, (c + 1) * crow // BLOCK, functools.partial(mem_values, h), 0
            )
            mine = att.at[h, pl.ds(c * crow, crow)]
            for m in others + [1]:
                copy = pltpu.make_async_remote_copy(
                    src_ref=mine, dst_ref=att_place(tme, h, c), send_sem=a_ss.at[h, c, m],
                    recv_sem=a_rs.at[h, c, m], device_id={"tensor": flipped(tme, m)},
                    device_id_type=MESH,
                )
                copy.start()
                a_copies[h, c, m] = copy
            own = pltpu.make_async_copy(
                mine, att_place(tme, h, c), own_sem.at[2 + h * chunks + c]
            )
            own.start()
            own_copies.append(own)
    forward(heads - 1)

    for h in range(heads):
        for c in range(chunks):
            a_copies[h, c, 1].wait_recv()
    for copy in f_copies:
        copy.wait()
    for copy in a_copies.values():
        copy.wait_send()
    for copy in w_copies:
        copy.wait()
    for copies in k_copies + v_copies:
        for copy in copies:
            copy.wait_send()
    for copy in own_copies:
        copy.wait()


def request_plan(retrieved, block_slot, local_blocks, peer_count):
    wanted = retrieved.reshape(-1)
    count = wanted.shape[0]
    table_ids = jnp.arange(block_slot.shape[0], dtype=jnp.int32)
    slot = jnp.sum(
        jnp.where(wanted[:, None] == table_ids[None, :], block_slot[None, :], 0), axis=1
    )
    owner = slot // local_blocks
    number = jnp.arange(count, dtype=jnp.int32)
    same = slot[:, None] == slot[None, :]
    first = jnp.min(jnp.where(same, number[None, :], count), axis=1)
    leads = first == number
    before = (
        leads[None, :] & (owner[:, None] == owner[None, :]) & (number[None, :] < first[:, None])
    )
    position = jnp.sum(before.astype(jnp.int32), axis=1)
    peer_ids = jnp.arange(peer_count, dtype=jnp.int32)
    lanes = jnp.arange(128, dtype=jnp.int32)
    match = (owner[:, None, None] == peer_ids[None, :, None]) & (
        position[:, None, None] == lanes[None, None, :]
    )
    request = jnp.max(jnp.where(match, (slot % local_blocks)[:, None, None], 0), axis=0)
    return jnp.stack([owner, position]), request


def shards(
    queries, keys, values, mem_keys, mem_values, gate_bias, out_weight, retrieved, block_slot
):
    tok, width = queries.shape
    heads = gate_bias.shape[0]
    head = width // heads
    peers = lax.axis_size("dp")
    groups = lax.axis_size("tensor")
    local_blocks = mem_keys.shape[0] // BLOCK
    feats = out_weight.shape[1] // groups
    chunks = tok // 256
    place, request = request_plan(retrieved, block_slot, local_blocks, peers)
    request = jnp.broadcast_to(request[:, None, :], (peers, 8, 128))
    gate_row = jnp.repeat(jax.nn.sigmoid(gate_bias), head)[None, :]
    sliced = feats % 128 == 0
    weight = out_weight
    if not sliced:
        weight = out_weight.reshape(width, groups, feats).transpose(1, 0, 2)
    blocked = (local_blocks, BLOCK, width)
    bf16 = jnp.bfloat16
    landing = pltpu.VMEM((peers, UNIQ_CAP, BLOCK, head), bf16)
    dma = pltpu.SemaphoreType.DMA
    any_spec = pl.BlockSpec(memory_space=pltpu.HBM)
    gathered, weights = pl.pallas_call(
        functools.partial(layer_kernel, peers, groups, heads, sliced),
        out_shape=(
            jax.ShapeDtypeStruct((tok, groups * width), bf16),
            jax.ShapeDtypeStruct((groups * width, feats), bf16),
        ),
        in_specs=[
            pl.BlockSpec(memory_space=pltpu.SMEM),
            pl.BlockSpec(memory_space=pltpu.VMEM),
            pl.BlockSpec(memory_space=pltpu.VMEM),
        ]
        + [any_spec] * 6,
        out_specs=(any_spec, any_spec),
        scratch_shapes=[
            pltpu.VMEM((tok, width), bf16),
            pltpu.VMEM((tok, width), bf16),
            pltpu.VMEM((tok, width), bf16),
            pltpu.VMEM(blocked, bf16),
            pltpu.VMEM(blocked, bf16),
            pltpu.VMEM((peers, 8, 128), jnp.int32),
            pltpu.SMEM((peers, 8, 128), jnp.int32),
            pltpu.VMEM((heads, peers, UNIQ_CAP, BLOCK, head), bf16),
            pltpu.VMEM((heads, peers, UNIQ_CAP, BLOCK, head), bf16),
            tuple(landing for _ in range(heads)),
            tuple(landing for _ in range(heads)),
            pltpu.VMEM((tok // BLOCK, BLOCK, TOPK * BLOCK), bf16),
            pltpu.VMEM((tok, head), jnp.float32),
            pltpu.VMEM((tok, width), jnp.float32),
            pltpu.VMEM((heads, tok, head), bf16),
            dma((5,)),
            dma(()),
            dma((2 + heads * chunks,)),
            dma((peers,)),
            dma((peers,)),
            dma((heads, peers)),
            dma((heads, peers)),
            dma((heads, peers)),
            dma((heads, peers)),
            dma((groups,)),
            dma((groups,)),
            dma((heads, chunks, groups)),
            dma((heads, chunks, groups)),
            dma((heads, chunks, groups)),
            dma((heads, chunks, groups)),
        ],
        compiler_params=pltpu.CompilerParams(
            collective_id=0, has_side_effects=True, vmem_limit_bytes=52 * 2**20
        ),
        name="memory_layer",
    )(
        place, request, gate_row, queries, keys, values,
        mem_keys.reshape(blocked), mem_values.reshape(blocked), weight,
    )
    return lax.dot_general(
        weights, gathered, (((0,), (1,)), ((), ())), preferred_element_type=jnp.float32
    ).astype(bf16)


def solution(mesh):
    in_specs = (
        P("dp", "tensor"),
        P("dp", "tensor"),
        P("dp", "tensor"),
        P("dp", "tensor"),
        P("dp", "tensor"),
        P("tensor"),
        P("tensor", None),
        P("dp", None),
        P(),
    )
    out_specs = P("tensor", "dp")
    return jax.shard_map(shards, mesh=mesh, in_specs=in_specs, out_specs=out_specs, check_vma=False)
```

```python
import functools
import math

import jax
import jax.numpy as jnp
from jax import lax
from jax.experimental import pallas as pl
from jax.experimental.pallas import tpu as pltpu
from jax.sharding import PartitionSpec as P

BLOCK = 128
SEG = 512
TOPK = 4
UNIQ_CAP = 4
MESH = pl.DeviceIdType.MESH
NT = (((1,), (1,)), ((), ()))


def flipped(index, mask):
    bit = 1
    result = index
    while bit <= mask:
        if mask & bit:
            result = result + bit * (1 - 2 * (lax.rem(lax.div(index, bit), 2)))
        bit *= 2
    return result


def layer_kernel(
    peers, groups, heads, sliced,
    place_ref, req_ref, gate_ref, q_hbm, k_hbm, v_hbm, mk_hbm, mv_hbm, w_hbm,
    ag_hbm, wg_hbm, part_hbm,
    q_vm, k_vm, v_vm, mk_vm, mv_vm, req_in, req_sm, send_k, send_v, recv_k, recv_v,
    probs, coef, local, att, ag_vm, wg_vm, part_vm,
    in_sem, smem_sem, own_sem, own_w_sem, req_ss, req_rs, k_ss, k_rs, v_ss, v_rs, w_ss, w_rs,
    a_ss, a_rs, f_ss, f_rs, part_sem,
):
    me = lax.axis_index("dp")
    tme = lax.axis_index("tensor")
    tok, width = q_vm.shape
    head = width // heads
    feats = wg_hbm.shape[1]
    scale = head ** -0.5 * math.log2(math.e)
    chunks = a_ss.shape[1]
    crow = tok // chunks

    loads = [
        pltpu.make_async_copy(src, dst, in_sem.at[i])
        for i, (src, dst) in enumerate(
            ((mk_hbm, mk_vm), (mv_hbm, mv_vm), (q_hbm, q_vm), (k_hbm, k_vm), (v_hbm, v_vm))
        )
    ]
    for load in loads:
        load.start()

    barrier = pltpu.get_barrier_semaphore()
    for m in range(1, peers):
        pl.semaphore_signal(barrier, inc=1, device_id={"dp": flipped(me, m)}, device_id_type=MESH)
    for m in range(1, groups):
        pl.semaphore_signal(
            barrier, inc=1, device_id={"tensor": flipped(tme, m)}, device_id_type=MESH
        )
    pl.semaphore_wait(barrier, peers - 1 + groups - 1)

    order = list(range(peers // 2, peers)) + list(range(peers // 2 - 1, 0, -1))

    req_copies = []
    for m in order:
        peer = flipped(me, m)
        copy = pltpu.make_async_remote_copy(
            src_ref=req_ref.at[peer], dst_ref=req_in.at[m], send_sem=req_ss.at[m],
            recv_sem=req_rs.at[m], device_id={"dp": peer}, device_id_type=MESH,
        )
        copy.start()
        req_copies.append(copy)

    def weight_part(t, h):
        rows = pl.ds(h * head, head)
        if sliced:
            return w_hbm.at[rows, pl.ds(pl.multiple_of(t * feats, 128), feats)]
        return w_hbm.at[t, rows]

    def weight_place(t, h):
        if h < heads - 1:
            column = pl.multiple_of(h * groups * head + t * head, 128)
            return wg_vm.at[pl.ds(column, head)]
        return wg_hbm.at[pl.ds(pl.multiple_of(t * head, 128), head)]

    w_copies, own_w = [], []
    for h in range(heads):
        for m in range(1, groups):
            peer = flipped(tme, m)
            copy = pltpu.make_async_remote_copy(
                src_ref=weight_part(peer, h), dst_ref=weight_place(tme, h),
                send_sem=w_ss.at[h, m], recv_sem=w_rs.at[h, m], device_id={"tensor": peer},
                device_id_type=MESH,
            )
            copy.start()
            w_copies.append(copy)
        own = pltpu.make_async_copy(weight_part(tme, h), weight_place(tme, h), own_w_sem.at[h])
        own.start()
        own_w.append(own)

    own_req = pltpu.make_async_copy(req_ref.at[me], req_in.at[0], own_sem.at[0])
    own_req.start()
    own_req.wait()
    for copy in req_copies:
        copy.wait()
    to_smem = pltpu.make_async_copy(req_in, req_sm, smem_sem)
    to_smem.start()
    loads[0].wait()
    to_smem.wait()

    def ship(source, h, send, recv, ss, rs):
        copies = []
        cols = slice(h * head, (h + 1) * head)
        for m in order:
            peer = flipped(me, m)
            for c in range(UNIQ_CAP):
                send[h, m, c] = source[req_sm[m, 0, c], :, cols]
            copy = pltpu.make_async_remote_copy(
                src_ref=send.at[h, m], dst_ref=recv[h].at[me], send_sem=ss.at[h, m],
                recv_sem=rs.at[h, m], device_id={"dp": peer}, device_id_type=MESH,
            )
            copy.start()
            copies.append(copy)
        for c in range(UNIQ_CAP):
            recv[h][me, c] = source[req_sm[0, 0, c], :, cols]
        return copies

    shipped = []

    def ship_next():
        stage = len(shipped)
        h = stage // 2
        if stage % 2 == 0:
            shipped.append(ship(mk_vm, h, send_k, recv_k, k_ss, k_rs))
        else:
            shipped.append(ship(mv_vm, h, send_v, recv_v, v_ss, v_rs))

    def follow(stage):
        for copy in shipped[stage]:
            copy.wait_send()
        if len(shipped) < 2 * heads:
            ship_next()
        for copy in shipped[stage]:
            copy.wait_recv()

    ship_next()
    loads[1].wait()
    ship_next()
    for load in loads[2:]:
        load.wait()

    blocks_seg = SEG // BLOCK

    def local_segment(s, carry):
        base = pl.multiple_of(s * SEG, SEG)
        for h in range(heads):
            cols = slice(h * head, (h + 1) * head)
            gate = gate_ref[:, cols]
            for i in range(blocks_seg):
                span = (i + 1) * BLOCK
                rows = pl.ds(pl.multiple_of(base + i * BLOCK, BLOCK), BLOCK)
                scores = lax.dot_general(
                    q_vm[rows, cols], k_vm[pl.ds(base, span), cols], NT,
                    preferred_element_type=jnp.float32,
                )
                row = lax.broadcasted_iota(jnp.int32, (BLOCK, span), 0) + i * BLOCK
                col = lax.broadcasted_iota(jnp.int32, (BLOCK, span), 1)
                scores = jnp.where(col <= row, scores, -jnp.inf)
                top = jnp.max(scores, axis=1, keepdims=True)
                weights = jnp.exp2((scores - top) * scale)
                total = jnp.sum(weights, axis=1, keepdims=True)
                out = jnp.dot(
                    weights.astype(jnp.bfloat16), v_vm[pl.ds(base, span), cols],
                    preferred_element_type=jnp.float32,
                )
                local[rows, cols] = out * ((1.0 - gate) / total)
        return carry

    lax.fori_loop(0, tok // SEG, local_segment, 0)

    def fetched(recv, h, b):
        return jnp.concatenate(
            [
                recv[h][place_ref[0, b * TOPK + j], place_ref[1, b * TOPK + j]]
                for j in range(TOPK)
            ],
            axis=0,
        )

    def mem_scores(h, b, carry):
        rows = pl.ds(pl.multiple_of(b * BLOCK, BLOCK), BLOCK)
        cols = slice(h * head, (h + 1) * head)
        scores = lax.dot_general(
            q_vm[rows, cols], fetched(recv_k, h, b), NT, preferred_element_type=jnp.float32
        )
        top = jnp.max(scores, axis=1, keepdims=True)
        weights = jnp.exp2((scores - top) * scale)
        total = jnp.sum(weights, axis=1, keepdims=True)
        probs[b] = weights.astype(jnp.bfloat16)
        coef[rows, :] = gate_ref[:, cols] / total
        return carry

    def mem_values(h, b, carry):
        rows = pl.ds(pl.multiple_of(b * BLOCK, BLOCK), BLOCK)
        cols = slice(h * head, (h + 1) * head)
        out = jnp.dot(probs[b], fetched(recv_v, h, b), preferred_element_type=jnp.float32)
        att[h, rows, :] = (coef[rows, :] * out + local[rows, cols]).astype(att.dtype)
        return carry

    def att_place(t, h, c):
        column = pl.multiple_of(t * head, 128)
        if h < heads - 1:
            column = pl.multiple_of(h * groups * head + t * head, 128)
            return ag_vm.at[pl.ds(c * crow, crow), pl.ds(column, head)]
        return ag_hbm.at[pl.ds(c * crow, crow), pl.ds(column, head)]

    mate = flipped(tme, 1)
    others = list(range(2, groups, 2))
    a_copies, f_copies, own_copies = {}, {}, {}

    def forward(h):
        for c in range(chunks):
            for m in others:
                a_copies[h, c, m].wait_recv()
                part = att_place(flipped(tme, m), h, c)
                copy = pltpu.make_async_remote_copy(
                    src_ref=part, dst_ref=part, send_sem=f_ss.at[h, c, m],
                    recv_sem=f_rs.at[h, c, m], device_id={"tensor": mate}, device_id_type=MESH,
                )
                copy.start()
                f_copies[h, c, m] = copy

    def settle(h):
        for c in range(chunks):
            a_copies[h, c, 1].wait_recv()
            for m in others:
                f_copies[h, c, m].wait()
            for m in others + [1]:
                a_copies[h, c, m].wait_send()
            own_copies[h, c].wait()

    tile = 256 if feats % 256 == 0 else feats

    def project(i, carry):
        at = pl.ds(pl.multiple_of(i * tile, tile), tile) if tile < feats else slice(None)
        out = lax.dot_general(
            wg_vm[:, at], ag_vm[...], (((0,), (1,)), ((), ())),
            preferred_element_type=jnp.float32,
        )
        part_vm[at, :] = out.astype(part_vm.dtype)
        return carry

    for h in range(heads):
        follow(2 * h)
        lax.fori_loop(0, tok // BLOCK, functools.partial(mem_scores, h), 0)
        if h > 0:
            forward(h - 1)
        if h == heads - 1:
            for early in range(heads - 1):
                settle(early)
            for copy in w_copies + own_w:
                copy.wait()
            lax.fori_loop(0, feats // tile, project, 0)
            part_copy = pltpu.make_async_copy(part_vm, part_hbm, part_sem)
            part_copy.start()
        follow(2 * h + 1)
        for c in range(chunks):
            lax.fori_loop(
                c * crow // BLOCK, (c + 1) * crow // BLOCK, functools.partial(mem_values, h), 0
            )
            mine = att.at[h, pl.ds(c * crow, crow)]
            for m in others + [1]:
                copy = pltpu.make_async_remote_copy(
                    src_ref=mine, dst_ref=att_place(tme, h, c), send_sem=a_ss.at[h, c, m],
                    recv_sem=a_rs.at[h, c, m], device_id={"tensor": flipped(tme, m)},
                    device_id_type=MESH,
                )
                copy.start()
                a_copies[h, c, m] = copy
            own = pltpu.make_async_copy(
                mine, att_place(tme, h, c), own_sem.at[1 + h * chunks + c]
            )
            own.start()
            own_copies[h, c] = own
    forward(heads - 1)
    settle(heads - 1)
    part_copy.wait()


def request_plan(retrieved, block_slot, local_blocks, peer_count):
    wanted = retrieved.reshape(-1)
    count = wanted.shape[0]
    table_ids = jnp.arange(block_slot.shape[0], dtype=jnp.int32)
    slot = jnp.sum(
        jnp.where(wanted[:, None] == table_ids[None, :], block_slot[None, :], 0), axis=1
    )
    owner = slot // local_blocks
    number = jnp.arange(count, dtype=jnp.int32)
    same = slot[:, None] == slot[None, :]
    first = jnp.min(jnp.where(same, number[None, :], count), axis=1)
    leads = first == number
    before = (
        leads[None, :] & (owner[:, None] == owner[None, :]) & (number[None, :] < first[:, None])
    )
    position = jnp.sum(before.astype(jnp.int32), axis=1)
    peer_ids = jnp.arange(peer_count, dtype=jnp.int32)
    lanes = jnp.arange(128, dtype=jnp.int32)
    match = (owner[:, None, None] == peer_ids[None, :, None]) & (
        position[:, None, None] == lanes[None, None, :]
    )
    request = jnp.max(jnp.where(match, (slot % local_blocks)[:, None, None], 0), axis=0)
    return jnp.stack([owner, position]), request


def shards(
    queries, keys, values, mem_keys, mem_values, gate_bias, out_weight, retrieved, block_slot
):
    tok, width = queries.shape
    heads = gate_bias.shape[0]
    head = width // heads
    peers = lax.axis_size("dp")
    groups = lax.axis_size("tensor")
    local_blocks = mem_keys.shape[0] // BLOCK
    feats = out_weight.shape[1] // groups
    chunks = tok // 256
    place, request = request_plan(retrieved, block_slot, local_blocks, peers)
    request = jnp.broadcast_to(request[:, None, :], (peers, 8, 128))
    gate_row = jnp.repeat(jax.nn.sigmoid(gate_bias), head)[None, :]
    sliced = feats % 128 == 0
    weight = out_weight
    if not sliced:
        weight = out_weight.reshape(width, groups, feats).transpose(1, 0, 2)
    blocked = (local_blocks, BLOCK, width)
    bf16 = jnp.bfloat16
    early = (heads - 1) * groups * head
    landing = pltpu.VMEM((peers, UNIQ_CAP, BLOCK, head), bf16)
    dma = pltpu.SemaphoreType.DMA
    any_spec = pl.BlockSpec(memory_space=pltpu.HBM)
    gathered, weights, partial = pl.pallas_call(
        functools.partial(layer_kernel, peers, groups, heads, sliced),
        out_shape=(
            jax.ShapeDtypeStruct((tok, groups * head), bf16),
            jax.ShapeDtypeStruct((groups * head, feats), bf16),
            jax.ShapeDtypeStruct((feats, tok), bf16),
        ),
        in_specs=[
            pl.BlockSpec(memory_space=pltpu.SMEM),
            pl.BlockSpec(memory_space=pltpu.VMEM),
            pl.BlockSpec(memory_space=pltpu.VMEM),
        ]
        + [any_spec] * 6,
        out_specs=(any_spec, any_spec, any_spec),
        scratch_shapes=[
            pltpu.VMEM((tok, width), bf16),
            pltpu.VMEM((tok, width), bf16),
            pltpu.VMEM((tok, width), bf16),
            pltpu.VMEM(blocked, bf16),
            pltpu.VMEM(blocked, bf16),
            pltpu.VMEM((peers, 8, 128), jnp.int32),
            pltpu.SMEM((peers, 8, 128), jnp.int32),
            pltpu.VMEM((heads, peers, UNIQ_CAP, BLOCK, head), bf16),
            pltpu.VMEM((heads, peers, UNIQ_CAP, BLOCK, head), bf16),
            tuple(landing for _ in range(heads)),
            tuple(landing for _ in range(heads)),
            pltpu.VMEM((tok // BLOCK, BLOCK, TOPK * BLOCK), bf16),
            pltpu.VMEM((tok, head), jnp.float32),
            pltpu.VMEM((tok, width), jnp.float32),
            pltpu.VMEM((heads, tok, head), bf16),
            pltpu.VMEM((tok, early), bf16),
            pltpu.VMEM((early, feats), bf16),
            pltpu.VMEM((feats, tok), bf16),
            dma((5,)),
            dma(()),
            dma((1 + heads * chunks,)),
            dma((heads,)),
            dma((peers,)),
            dma((peers,)),
            dma((heads, peers)),
            dma((heads, peers)),
            dma((heads, peers)),
            dma((heads, peers)),
            dma((heads, groups)),
            dma((heads, groups)),
            dma((heads, chunks, groups)),
            dma((heads, chunks, groups)),
            dma((heads, chunks, groups)),
            dma((heads, chunks, groups)),
            dma(()),
        ],
        compiler_params=pltpu.CompilerParams(
            collective_id=0, has_side_effects=True, vmem_limit_bytes=62 * 2**20
        ),
        name="memory_layer",
    )(
        place, request, gate_row, queries, keys, values,
        mem_keys.reshape(blocked), mem_values.reshape(blocked), weight,
    )
    late = lax.dot_general(
        weights, gathered, (((0,), (1,)), ((), ())), preferred_element_type=jnp.float32
    )
    return (late + partial.astype(jnp.float32)).astype(bf16)


def solution(mesh):
    in_specs = (
        P("dp", "tensor"),
        P("dp", "tensor"),
        P("dp", "tensor"),
        P("dp", "tensor"),
        P("dp", "tensor"),
        P("tensor"),
        P("tensor", None),
        P("dp", None),
        P(),
    )
    out_specs = P("tensor", "dp")
    return jax.shard_map(shards, mesh=mesh, in_specs=in_specs, out_specs=out_specs, check_vma=False)
```

```python
import functools
import math

import jax
import jax.numpy as jnp
from jax import lax
from jax.experimental import pallas as pl
from jax.experimental.pallas import tpu as pltpu
from jax.sharding import PartitionSpec as P

BLOCK = 128
SEG = 512
TOPK = 4
UNIQ_CAP = 4
MESH = pl.DeviceIdType.MESH
NT = (((1,), (1,)), ((), ()))


def flipped(index, mask):
    bit = 1
    result = index
    while bit <= mask:
        if mask & bit:
            result = result + bit * (1 - 2 * (lax.rem(lax.div(index, bit), 2)))
        bit *= 2
    return result


def layer_kernel(
    peers, groups, heads, sliced,
    place_ref, req_ref, gate_ref, q_hbm, k_hbm, v_hbm, mk_hbm, mv_hbm, w_hbm,
    ag_hbm, wg_hbm, part_hbm,
    q_vm, k_vm, v_vm, mk_vm, mv_vm, req_in, req_sm, send_k, send_v, recv_k, recv_v,
    probs, coef, local, att, ag_vm, wg_vm, part_vm,
    in_sem, smem_sem, own_sem, own_w_sem, req_ss, req_rs, k_ss, k_rs, v_ss, v_rs, w_ss, w_rs,
    a_ss, a_rs, f_ss, f_rs, part_sem,
):
    me = lax.axis_index("dp")
    tme = lax.axis_index("tensor")
    tok, width = q_vm.shape
    head = width // heads
    feats = wg_hbm.shape[1]
    scale = head ** -0.5 * math.log2(math.e)
    chunks = a_ss.shape[1]
    crow = tok // chunks

    loads = [
        pltpu.make_async_copy(src, dst, in_sem.at[i])
        for i, (src, dst) in enumerate(
            ((mk_hbm, mk_vm), (mv_hbm, mv_vm), (q_hbm, q_vm), (k_hbm, k_vm), (v_hbm, v_vm))
        )
    ]
    for load in loads:
        load.start()

    barrier = pltpu.get_barrier_semaphore()
    for m in range(1, peers):
        pl.semaphore_signal(barrier, inc=1, device_id={"dp": flipped(me, m)}, device_id_type=MESH)
    for m in range(1, groups):
        pl.semaphore_signal(
            barrier, inc=1, device_id={"tensor": flipped(tme, m)}, device_id_type=MESH
        )
    pl.semaphore_wait(barrier, peers - 1 + groups - 1)

    order = list(range(1, peers))

    req_copies = []
    for m in order:
        peer = flipped(me, m)
        copy = pltpu.make_async_remote_copy(
            src_ref=req_ref.at[peer], dst_ref=req_in.at[m], send_sem=req_ss.at[m],
            recv_sem=req_rs.at[m], device_id={"dp": peer}, device_id_type=MESH,
        )
        copy.start()
        req_copies.append(copy)

    def weight_part(t, h):
        rows = pl.ds(h * head, head)
        if sliced:
            return w_hbm.at[rows, pl.ds(pl.multiple_of(t * feats, 128), feats)]
        return w_hbm.at[t, rows]

    def weight_place(t, h):
        if h < heads - 1:
            column = pl.multiple_of(h * groups * head + t * head, 128)
            return wg_vm.at[pl.ds(column, head)]
        return wg_hbm.at[pl.ds(pl.multiple_of(t * head, 128), head)]

    w_copies, own_w = [], []
    for h in range(heads):
        for m in range(1, groups):
            peer = flipped(tme, m)
            copy = pltpu.make_async_remote_copy(
                src_ref=weight_part(peer, h), dst_ref=weight_place(tme, h),
                send_sem=w_ss.at[h, m], recv_sem=w_rs.at[h, m], device_id={"tensor": peer},
                device_id_type=MESH,
            )
            copy.start()
            w_copies.append(copy)
        own = pltpu.make_async_copy(weight_part(tme, h), weight_place(tme, h), own_w_sem.at[h])
        own.start()
        own_w.append(own)

    own_req = pltpu.make_async_copy(req_ref.at[me], req_in.at[0], own_sem.at[0])
    own_req.start()
    own_req.wait()
    for copy in req_copies:
        copy.wait()
    to_smem = pltpu.make_async_copy(req_in, req_sm, smem_sem)
    to_smem.start()
    loads[0].wait()
    to_smem.wait()

    def ship(source, h, send, recv, ss, rs):
        copies = []
        cols = slice(h * head, (h + 1) * head)
        for m in order:
            peer = flipped(me, m)
            for c in range(UNIQ_CAP):
                send[h, m, c] = source[req_sm[m, 0, c], :, cols]
            copy = pltpu.make_async_remote_copy(
                src_ref=send.at[h, m], dst_ref=recv[h].at[me], send_sem=ss.at[h, m],
                recv_sem=rs.at[h, m], device_id={"dp": peer}, device_id_type=MESH,
            )
            copy.start()
            copies.append(copy)
        for c in range(UNIQ_CAP):
            recv[h][me, c] = source[req_sm[0, 0, c], :, cols]
        return copies

    shipped = []

    def ship_next():
        stage = len(shipped)
        h = stage // 2
        if stage % 2 == 0:
            shipped.append(ship(mk_vm, h, send_k, recv_k, k_ss, k_rs))
        else:
            shipped.append(ship(mv_vm, h, send_v, recv_v, v_ss, v_rs))

    def follow(stage):
        for copy in shipped[stage]:
            copy.wait_send()
        if len(shipped) < 2 * heads:
            ship_next()
        for copy in shipped[stage]:
            copy.wait_recv()

    ship_next()
    loads[1].wait()
    ship_next()
    for load in loads[2:]:
        load.wait()

    blocks_seg = SEG // BLOCK

    def local_segment(s, carry):
        base = pl.multiple_of(s * SEG, SEG)
        for h in range(heads):
            cols = slice(h * head, (h + 1) * head)
            gate = gate_ref[:, cols]
            for i in range(blocks_seg):
                span = (i + 1) * BLOCK
                rows = pl.ds(pl.multiple_of(base + i * BLOCK, BLOCK), BLOCK)
                scores = lax.dot_general(
                    q_vm[rows, cols], k_vm[pl.ds(base, span), cols], NT,
                    preferred_element_type=jnp.float32,
                )
                row = lax.broadcasted_iota(jnp.int32, (BLOCK, span), 0) + i * BLOCK
                col = lax.broadcasted_iota(jnp.int32, (BLOCK, span), 1)
                scores = jnp.where(col <= row, scores, -jnp.inf)
                top = jnp.max(scores, axis=1, keepdims=True)
                weights = jnp.exp2((scores - top) * scale)
                total = jnp.sum(weights, axis=1, keepdims=True)
                out = jnp.dot(
                    weights.astype(jnp.bfloat16), v_vm[pl.ds(base, span), cols],
                    preferred_element_type=jnp.float32,
                )
                local[rows, cols] = out * ((1.0 - gate) / total)
        return carry

    lax.fori_loop(0, tok // SEG, local_segment, 0)

    def fetched(recv, h, b):
        return jnp.concatenate(
            [
                recv[h][place_ref[0, b * TOPK + j], place_ref[1, b * TOPK + j]]
                for j in range(TOPK)
            ],
            axis=0,
        )

    def mem_scores(h, b, carry):
        rows = pl.ds(pl.multiple_of(b * BLOCK, BLOCK), BLOCK)
        cols = slice(h * head, (h + 1) * head)
        scores = lax.dot_general(
            q_vm[rows, cols], fetched(recv_k, h, b), NT, preferred_element_type=jnp.float32
        )
        top = jnp.max(scores, axis=1, keepdims=True)
        weights = jnp.exp2((scores - top) * scale)
        total = jnp.sum(weights, axis=1, keepdims=True)
        probs[b] = weights.astype(jnp.bfloat16)
        coef[rows, :] = gate_ref[:, cols] / total
        return carry

    def mem_values(h, b, carry):
        rows = pl.ds(pl.multiple_of(b * BLOCK, BLOCK), BLOCK)
        cols = slice(h * head, (h + 1) * head)
        out = jnp.dot(probs[b], fetched(recv_v, h, b), preferred_element_type=jnp.float32)
        att[h, rows, :] = (coef[rows, :] * out + local[rows, cols]).astype(att.dtype)
        return carry

    def att_place(t, h, c):
        column = pl.multiple_of(t * head, 128)
        if h < heads - 1:
            column = pl.multiple_of(h * groups * head + t * head, 128)
            return ag_vm.at[pl.ds(c * crow, crow), pl.ds(column, head)]
        return ag_hbm.at[pl.ds(c * crow, crow), pl.ds(column, head)]

    mate = flipped(tme, 1)
    others = list(range(2, groups, 2))
    a_copies, f_copies, own_copies = {}, {}, {}

    def forward(h):
        for c in range(chunks):
            for m in others:
                a_copies[h, c, m].wait_recv()
                part = att_place(flipped(tme, m), h, c)
                copy = pltpu.make_async_remote_copy(
                    src_ref=part, dst_ref=part, send_sem=f_ss.at[h, c, m],
                    recv_sem=f_rs.at[h, c, m], device_id={"tensor": mate}, device_id_type=MESH,
                )
                copy.start()
                f_copies[h, c, m] = copy

    def settle(h):
        for c in range(chunks):
            a_copies[h, c, 1].wait_recv()
            for m in others:
                f_copies[h, c, m].wait()
            for m in others + [1]:
                a_copies[h, c, m].wait_send()
            own_copies[h, c].wait()

    tile = 256 if feats % 256 == 0 else feats

    def project(i, carry):
        at = pl.ds(pl.multiple_of(i * tile, tile), tile) if tile < feats else slice(None)
        out = lax.dot_general(
            wg_vm[:, at], ag_vm[...], (((0,), (1,)), ((), ())),
            preferred_element_type=jnp.float32,
        )
        part_vm[at, :] = out.astype(part_vm.dtype)
        return carry

    for h in range(heads):
        follow(2 * h)
        lax.fori_loop(0, tok // BLOCK, functools.partial(mem_scores, h), 0)
        if h > 0:
            forward(h - 1)
        if h == heads - 1:
            for early in range(heads - 1):
                settle(early)
            for copy in w_copies + own_w:
                copy.wait()
            lax.fori_loop(0, feats // tile, project, 0)
            part_copy = pltpu.make_async_copy(part_vm, part_hbm, part_sem)
            part_copy.start()
        follow(2 * h + 1)
        for c in range(chunks):
            lax.fori_loop(
                c * crow // BLOCK, (c + 1) * crow // BLOCK, functools.partial(mem_values, h), 0
            )
            mine = att.at[h, pl.ds(c * crow, crow)]
            for m in others + [1]:
                copy = pltpu.make_async_remote_copy(
                    src_ref=mine, dst_ref=att_place(tme, h, c), send_sem=a_ss.at[h, c, m],
                    recv_sem=a_rs.at[h, c, m], device_id={"tensor": flipped(tme, m)},
                    device_id_type=MESH,
                )
                copy.start()
                a_copies[h, c, m] = copy
            own = pltpu.make_async_copy(
                mine, att_place(tme, h, c), own_sem.at[1 + h * chunks + c]
            )
            own.start()
            own_copies[h, c] = own
    forward(heads - 1)
    settle(heads - 1)
    part_copy.wait()


def request_plan(retrieved, block_slot, local_blocks, peer_count):
    wanted = retrieved.reshape(-1)
    count = wanted.shape[0]
    table_ids = jnp.arange(block_slot.shape[0], dtype=jnp.int32)
    slot = jnp.sum(
        jnp.where(wanted[:, None] == table_ids[None, :], block_slot[None, :], 0), axis=1
    )
    owner = slot // local_blocks
    number = jnp.arange(count, dtype=jnp.int32)
    same = slot[:, None] == slot[None, :]
    first = jnp.min(jnp.where(same, number[None, :], count), axis=1)
    leads = first == number
    before = (
        leads[None, :] & (owner[:, None] == owner[None, :]) & (number[None, :] < first[:, None])
    )
    position = jnp.sum(before.astype(jnp.int32), axis=1)
    peer_ids = jnp.arange(peer_count, dtype=jnp.int32)
    lanes = jnp.arange(128, dtype=jnp.int32)
    match = (owner[:, None, None] == peer_ids[None, :, None]) & (
        position[:, None, None] == lanes[None, None, :]
    )
    request = jnp.max(jnp.where(match, (slot % local_blocks)[:, None, None], 0), axis=0)
    return jnp.stack([owner, position]), request


def shards(
    queries, keys, values, mem_keys, mem_values, gate_bias, out_weight, retrieved, block_slot
):
    tok, width = queries.shape
    heads = gate_bias.shape[0]
    head = width // heads
    peers = lax.axis_size("dp")
    groups = lax.axis_size("tensor")
    local_blocks = mem_keys.shape[0] // BLOCK
    feats = out_weight.shape[1] // groups
    chunks = tok // 256
    place, request = request_plan(retrieved, block_slot, local_blocks, peers)
    request = jnp.broadcast_to(request[:, None, :], (peers, 8, 128))
    gate_row = jnp.repeat(jax.nn.sigmoid(gate_bias), head)[None, :]
    sliced = feats % 128 == 0
    weight = out_weight
    if not sliced:
        weight = out_weight.reshape(width, groups, feats).transpose(1, 0, 2)
    blocked = (local_blocks, BLOCK, width)
    bf16 = jnp.bfloat16
    early = (heads - 1) * groups * head
    landing = pltpu.VMEM((peers, UNIQ_CAP, BLOCK, head), bf16)
    dma = pltpu.SemaphoreType.DMA
    any_spec = pl.BlockSpec(memory_space=pltpu.HBM)
    gathered, weights, partial = pl.pallas_call(
        functools.partial(layer_kernel, peers, groups, heads, sliced),
        out_shape=(
            jax.ShapeDtypeStruct((tok, groups * head), bf16),
            jax.ShapeDtypeStruct((groups * head, feats), bf16),
            jax.ShapeDtypeStruct((feats, tok), bf16),
        ),
        in_specs=[
            pl.BlockSpec(memory_space=pltpu.SMEM),
            pl.BlockSpec(memory_space=pltpu.VMEM),
            pl.BlockSpec(memory_space=pltpu.VMEM),
        ]
        + [any_spec] * 6,
        out_specs=(any_spec, any_spec, any_spec),
        scratch_shapes=[
            pltpu.VMEM((tok, width), bf16),
            pltpu.VMEM((tok, width), bf16),
            pltpu.VMEM((tok, width), bf16),
            pltpu.VMEM(blocked, bf16),
            pltpu.VMEM(blocked, bf16),
            pltpu.VMEM((peers, 8, 128), jnp.int32),
            pltpu.SMEM((peers, 8, 128), jnp.int32),
            pltpu.VMEM((heads, peers, UNIQ_CAP, BLOCK, head), bf16),
            pltpu.VMEM((heads, peers, UNIQ_CAP, BLOCK, head), bf16),
            tuple(landing for _ in range(heads)),
            tuple(landing for _ in range(heads)),
            pltpu.VMEM((tok // BLOCK, BLOCK, TOPK * BLOCK), bf16),
            pltpu.VMEM((tok, head), jnp.float32),
            pltpu.VMEM((tok, width), jnp.float32),
            pltpu.VMEM((heads, tok, head), bf16),
            pltpu.VMEM((tok, early), bf16),
            pltpu.VMEM((early, feats), bf16),
            pltpu.VMEM((feats, tok), bf16),
            dma((5,)),
            dma(()),
            dma((1 + heads * chunks,)),
            dma((heads,)),
            dma((peers,)),
            dma((peers,)),
            dma((heads, peers)),
            dma((heads, peers)),
            dma((heads, peers)),
            dma((heads, peers)),
            dma((heads, groups)),
            dma((heads, groups)),
            dma((heads, chunks, groups)),
            dma((heads, chunks, groups)),
            dma((heads, chunks, groups)),
            dma((heads, chunks, groups)),
            dma(()),
        ],
        compiler_params=pltpu.CompilerParams(
            collective_id=0, has_side_effects=True, vmem_limit_bytes=62 * 2**20
        ),
        name="memory_layer",
    )(
        place, request, gate_row, queries, keys, values,
        mem_keys.reshape(blocked), mem_values.reshape(blocked), weight,
    )
    late = lax.dot_general(
        weights, gathered, (((0,), (1,)), ((), ())), preferred_element_type=jnp.float32
    )
    return (late + partial.astype(jnp.float32)).astype(bf16)


def solution(mesh):
    in_specs = (
        P("dp", "tensor"),
        P("dp", "tensor"),
        P("dp", "tensor"),
        P("dp", "tensor"),
        P("dp", "tensor"),
        P("tensor"),
        P("tensor", None),
        P("dp", None),
        P(),
    )
    out_specs = P("tensor", "dp")
    return jax.shard_map(shards, mesh=mesh, in_specs=in_specs, out_specs=out_specs, check_vma=False)
```
